32 devices in a mesh: dp: 16 (over z, y, core), mp: 2 (over x).
Axes of the slice: x: 2, y: 2, z: 4, core: 2. Of those that a mesh axis runs over, the one named last changes fastest.
Arguments:
- tokens: bfloat16 [24576, 768], P('dp'), may hold values from -6 to 6
- window_length: int32 [48], P('dp'), may hold values from 128 to 512, as said below
- query_weight: bfloat16 [768, 768], P(None, 'mp'), may hold values from -0.21875 to 0.21875
- query_bias: bfloat16 [768], P('mp'), may hold values from -3 to 3
- key_weight: bfloat16 [768, 768], P(None, 'mp'), may hold values from -0.21875 to 0.21875
- value_weight: bfloat16 [768, 768], P(None, 'mp'), may hold values from -0.21875 to 0.21875
- value_bias: bfloat16 [768], P('mp'), may hold values from -3 to 3
- output_weight: bfloat16 [768, 768], P('mp'), may hold values from -2.5 to 2.5
- output_bias: bfloat16 [768], replicated, may hold values from -3 to 3
- first_gain: bfloat16 [768], replicated, may hold values from 0.099609375 to 1.8984375
- first_shift: bfloat16 [768], replicated, may hold values from -3 to 3
- inner_weight: bfloat16 [768, 3072], P(None, 'mp'), may hold values from -0.21875 to 0.21875
- inner_bias: bfloat16 [3072], P('mp'), may hold values from -3 to 3
- outer_weight: bfloat16 [3072, 768], P('mp'), may hold values from -0.109375 to 0.109375
- outer_bias: bfloat16 [768], replicated, may hold values from -3 to 3
- second_gain: bfloat16 [768], replicated, may hold values from 0.099609375 to 1.8984375
- second_shift: bfloat16 [768], replicated, may hold values from -3 to 3
- cotangent: bfloat16 [24576, 768], P(('dp', 'mp')), may hold values from -6 to 6
Outputs:
- layer_out: bfloat16 [24576, 768], P(('dp', 'mp'))
- tokens_grad: float32 [24576, 768], P(('dp', 'mp'))
- query_wgrad: float32 [768, 768], P(None, 'mp')
- query_bgrad: float32 [768], P('mp')
- key_wgrad: float32 [768, 768], P(None, 'mp')
- value_wgrad: float32 [768, 768], P(None, 'mp')
- value_bgrad: float32 [768], P('mp')
- output_wgrad: float32 [768, 768], P('mp')
- output_bgrad: float32 [768], replicated
- first_ggrad: float32 [768], replicated
- first_sgrad: float32 [768], replicated
- inner_wgrad: float32 [768, 3072], P(None, 'mp')
- inner_bgrad: float32 [3072], P('mp')
- outer_wgrad: float32 [3072, 768], P('mp')
- outer_bgrad: float32 [768], replicated
- second_ggrad: float32 [768], replicated
- second_sgrad: float32 [768], replicated
The draws below stay inside these ranges and needn't reach their ends.
Inputs may be any that keep to these rules, and one draw needn't show every extreme that they name: `window_length`: each entry is either 128 or 512; both occur.
All inputs are finite; a program needn't handle non-finite values.
Results may differ from the reference program's by a relative error of at most 0.018.
Values may be sent and summed in bfloat16 or wider, within the bound.
No kernel may reach another device: no remote copies, remote signals or barrier semaphores. Data moves between devices by JAX's collectives and lax.ppermute only.
A program may use at most 128 MiB of HBM per device.

```python
import jax
import jax.numpy as jnp
from jax import lax

D = 768
HEADS = 12
FF = 3072
HEAD = 64
SLOT = 512
SHORT = 128
WIN_DEV = 3
TOK_DEV = 1536
WINDOWS = 48
TOKENS = 24576


def draw_window_length(key, part):
    groups = WINDOWS // WIN_DEV
    rate_key = jax.random.fold_in(key, 11)
    roll_key = jax.random.fold_in(key, 23)
    rates = jax.random.randint(rate_key, (groups, 1), 0, 4)
    rolls = jax.random.randint(roll_key, (groups, WIN_DEV), 0, 3)
    longer = (rolls < rates).reshape(WINDOWS)
    longer = longer.at[0].set(True).at[1].set(False)
    return jnp.where(longer, SLOT, SHORT).astype(jnp.int32)


def shard_levels(rng, shape, shards, low, top_value):
    def one(dim, parts):
        draws = jax.random.uniform(jax.random.fold_in(jax.random.fold_in(rng, 6), dim), (parts,), jnp.float32, low / len(shards), top_value / len(shards))
        return jnp.repeat(jnp.exp(draws), shape[dim] // parts).reshape((-1,) + (1,) * (len(shape) - dim - 1))

    loudness = one(*shards[0])
    for cut in shards[1:]:
        loudness = loudness * one(*cut)
    return loudness


def gaussian(rng, dims, scale, limit, pieces=(), held_as=jnp.bfloat16):
    entries = scale * jax.random.normal(rng, dims, jnp.float32)
    if pieces:
        entries = entries * shard_levels(rng, dims, pieces, -0.22, 0.18)
    return jnp.clip(entries, -limit, limit).astype(held_as)


def setup_inputs(seed: int = 0) -> dict:
    splits = jax.random.split(jax.random.key(seed), 19)
    return {
        "tokens": gaussian(splits[0], (TOKENS, D), 1.0, 6.0, ((0, 16),)),
        "window_length": draw_window_length(jax.random.fold_in(splits[18], 71), 0),
        "query_weight": gaussian(splits[2], (D, D), D ** -0.5, 0.21875, ((1, 2),)),
        "query_bias": gaussian(splits[3], (D,), 0.5, 3.0, ((0, 2),)),
        "key_weight": gaussian(splits[4], (D, D), D ** -0.5, 0.21875, ((1, 2),)),
        "value_weight": gaussian(splits[5], (D, D), D ** -0.5, 0.21875, ((1, 2),)),
        "value_bias": gaussian(splits[6], (D,), 0.5, 3.0, ((0, 2),)),
        "output_weight": gaussian(splits[7], (D, D), (max(D // 128, 2)) ** -0.5, 2.5, ((0, 2),)),
        "output_bias": gaussian(splits[8], (D,), 0.5, 3.0),
        "first_gain": jnp.clip(1.0 + 0.18 * jax.random.normal(splits[9], (D,), jnp.float32), 0.099609375, 1.8984375).astype(jnp.bfloat16),
        "first_shift": gaussian(splits[10], (D,), 0.5, 3.0),
        "inner_weight": gaussian(splits[11], (D, FF), D ** -0.5, 0.21875, ((1, 2),)),
        "inner_bias": gaussian(splits[12], (FF,), 0.5, 3.0, ((0, 2),)),
        "outer_weight": gaussian(splits[13], (FF, D), FF ** -0.5, 0.109375, ((0, 2),)),
        "outer_bias": gaussian(splits[14], (D,), 0.5, 3.0),
        "second_gain": jnp.clip(1.0 + 0.18 * jax.random.normal(splits[15], (D,), jnp.float32), 0.099609375, 1.8984375).astype(jnp.bfloat16),
        "second_shift": gaussian(splits[16], (D,), 0.5, 3.0),
        "cotangent": gaussian(splits[17], (TOKENS, D), 1.0, 6.0, ((0, 32),)),
    }


@jax.custom_vjp
def low(v):
    return lax.optimization_barrier(v.astype(jnp.bfloat16)).astype(jnp.float32)

@jax.custom_vjp
def low_back(v):
    return v

def low_keep(v):
    return (low(v), None)

def low_pass(kept, grad):
    return (grad,)

def back_keep(v):
    return (v, None)

def back_low(kept, grad):
    return (low(grad),)
low.defvjp(low_keep, low_pass)
low_back.defvjp(back_keep, back_low)

def layer_norm(values, gain, shift):
    center = values - lax.optimization_barrier(jnp.mean(values, axis=-1, keepdims=True))
    spread = lax.optimization_barrier(jnp.mean(center * center, axis=-1, keepdims=True))
    return center * lax.rsqrt(spread + 1e-05) * gain + shift

def dense(left, right):
    return jnp.dot(left, right, precision=lax.Precision.HIGHEST)

def attend(block):
    queries, keys, values, length = block
    scale = HEAD ** (-0.5)
    scores = low_back(jnp.einsum('qhe,khe->hqk', queries, keys, precision=lax.Precision.HIGHEST) * scale)
    places = jnp.arange(SLOT, dtype=jnp.int32) // length
    allowed = places[:, None] == places[None, :]
    scores = jnp.where(allowed[None], scores, -1e+30)
    probs = low(jax.nn.softmax(scores, axis=-1))
    return jnp.einsum('hqk,khe->qhe', probs, values, precision=lax.Precision.HIGHEST)

def forward(params, inputs, lengths):
    query_weight, query_bias, key_weight, value_weight, value_bias, output_weight, output_bias, first_gain, first_shift, inner_weight, inner_bias, outer_weight, outer_bias, second_gain, second_shift = params
    count = inputs.shape[0]
    queries = low(low_back(dense(inputs, query_weight) + query_bias))
    keys = low(low_back(dense(inputs, key_weight)))
    values = low(low_back(dense(inputs, value_weight) + value_bias))
    split_shape = (count // SLOT, SLOT, HEADS, HEAD)
    mixed = lax.map(jax.checkpoint(attend), (queries.reshape(split_shape), keys.reshape(split_shape), values.reshape(split_shape), lengths))
    mixed = low(low_back(mixed.reshape(count, D)))
    first_in = inputs + low_back(dense(mixed, output_weight) + output_bias)
    normed = layer_norm(first_in, first_gain, first_shift)
    inner = low_back(dense(low(normed), inner_weight) + inner_bias)
    active = low(jax.nn.gelu(inner, approximate=True))
    second_in = normed + low_back(dense(active, outer_weight) + outer_bias)
    return layer_norm(second_in, second_gain, second_shift)

def reference(tokens, window_length, query_weight, query_bias, key_weight, value_weight, value_bias, output_weight, output_bias, first_gain, first_shift, inner_weight, inner_bias, outer_weight, outer_bias, second_gain, second_shift, cotangent):
    params = tuple((item.astype(jnp.float32) for item in (query_weight, query_bias, key_weight, value_weight, value_bias, output_weight, output_bias, first_gain, first_shift, inner_weight, inner_bias, outer_weight, outer_bias, second_gain, second_shift)))
    groups = TOKENS // TOK_DEV
    inputs_all = tokens.astype(jnp.float32).reshape(groups, TOK_DEV, D)
    cots_all = cotangent.astype(jnp.float32).reshape(groups, TOK_DEV, D)
    lengths_all = window_length.reshape(groups, TOK_DEV // SLOT)

    def step(total, block):
        inputs, cots, lengths = block
        result, pull = jax.vjp(lambda weights, values: forward(weights, values, lengths), params, inputs)
        param_grads, input_grads = pull(cots)
        total = jax.tree.map(lambda first, second: first + second, total, param_grads)
        return (total, (result.astype(jnp.bfloat16), input_grads))
    zeros = jax.tree.map(jnp.zeros_like, params)
    total, (results, input_grads) = lax.scan(step, zeros, (inputs_all, cots_all, lengths_all))
    return (results.reshape(TOKENS, D), input_grads.reshape(TOKENS, D), total[0], total[1], total[2], total[3], total[4], total[5], total[6], total[7], total[8], total[9], total[10], total[11], total[12], total[13], total[14])
```

```python
import jax
import jax.numpy as jnp
from jax import lax
from jax.experimental import pallas as pl
from jax.experimental.pallas import tpu as pltpu
from jax.sharding import PartitionSpec as P

HEAD = 64
LOW = jnp.bfloat16
F32 = jnp.float32


def mm(a, b, ca=1, cb=0):
    return lax.dot_general(a, b, (((ca,), (cb,)), ((), ())), preferred_element_type=F32)


def allowed_mask(length, slot):
    rows = lax.broadcasted_iota(jnp.int32, (slot, slot), 0)
    cols = lax.broadcasted_iota(jnp.int32, (slot, slot), 1)
    return (rows ^ cols) < length


def attend_kernel(info, tok, wq, wk, wv, bq, bv, q_ref, k_ref, v_ref, mix_ref, lse_ref, mixt):
    tokens = tok[...]
    q_ref[...] = (mm(tokens, wq[...]) + bq[...]).astype(LOW)
    k_ref[...] = mm(tokens, wk[...]).astype(LOW)
    v_ref[...] = (mm(tokens, wv[...]) + bv[...]).astype(LOW)
    slot, width = q_ref.shape
    length = info[1]
    scale = HEAD ** (-0.5)

    def heads(masked):
        allowed = allowed_mask(length, slot) if masked else None
        for h in range(width // HEAD):
            cut = slice(h * HEAD, (h + 1) * HEAD)
            scores = mm(k_ref[:, cut], q_ref[:, cut] * LOW(scale), 1, 1)
            if masked:
                scores = jnp.where(allowed, scores, -1e30)
            top = jnp.max(scores, axis=0, keepdims=True)
            weights = jnp.exp(scores - top)
            total = jnp.sum(weights, axis=0, keepdims=True)
            lse_ref[h : h + 1, :] = top + jnp.log(total)
            part = mm(v_ref[:, cut], weights.astype(LOW), 0, 0)
            mixt[cut, :] = part / total

    @pl.when(length < slot)
    def _():
        heads(True)

    @pl.when(length >= slot)
    def _():
        heads(False)

    mix_ref[...] = mixt[...].T.astype(LOW)


def attend(info, tokens, wq, wk, wv, bq, bv, slot):
    count, model = tokens.shape
    width = wq.shape[1]
    rows = (width // HEAD + 7) // 8 * 8
    full = lambda a: pl.BlockSpec(a.shape, lambda i, s: (0, 0))
    piece = lambda: pl.BlockSpec((slot, width), lambda i, s: (0, 0))
    return pl.pallas_call(
        attend_kernel,
        grid_spec=pltpu.PrefetchScalarGridSpec(
            num_scalar_prefetch=1,
            grid=(1,),
            in_specs=[pl.BlockSpec((slot, model), lambda i, s: (s[0], 0))]
            + [full(a) for a in (wq, wk, wv, bq, bv)],
            out_specs=[piece(), piece(), piece(), piece(), pl.BlockSpec((rows, slot), lambda i, s: (0, 0))],
            scratch_shapes=[pltpu.VMEM((width, slot), F32)],
        ),
        out_shape=[jax.ShapeDtypeStruct((slot, width), LOW)] * 4
        + [jax.ShapeDtypeStruct((rows, slot), F32)],
        cost_estimate=pl.CostEstimate(flops=4 * 10**9, transcendentals=2 * 10**6, bytes_accessed=4 * 10**6),
        name="attend",
    )(info, tokens, wq, wk, wv, bq, bv)


def attend_back_kernel(info, q_ref, k_ref, v_ref, lse_ref, do_ref, wq, wk, wv, prev, d_ref, dtok_ref, dqt):
    slot, width = q_ref.shape
    length = info[1]
    scale = HEAD ** (-0.5)

    def heads(masked):
        allowed = allowed_mask(length, slot) if masked else None
        for h in range(width // HEAD):
            cut = slice(h * HEAD, (h + 1) * HEAD)
            q = q_ref[:, cut] * LOW(scale)
            k = k_ref[:, cut]
            v = v_ref[:, cut]
            do = do_ref[:, cut]
            scores = mm(k, q, 1, 1)
            if masked:
                scores = jnp.where(allowed, scores, -1e30)
            probs = jnp.exp(scores - lse_ref[h : h + 1, :])
            dprobs = mm(v, do, 1, 1)
            inner = jnp.sum(probs * dprobs, axis=0, keepdims=True)
            ds = (probs * (dprobs - inner)).astype(LOW)
            d_ref[:, 2 * width + h * HEAD : 2 * width + (h + 1) * HEAD] = mm(probs.astype(LOW), do).astype(LOW)
            d_ref[:, width + h * HEAD : width + (h + 1) * HEAD] = mm(ds, q).astype(LOW)
            dqt[cut, :] = mm(k, ds, 0, 0) * scale

    @pl.when(length < slot)
    def _():
        heads(True)

    @pl.when(length >= slot)
    def _():
        heads(False)

    d_ref[:, :width] = dqt[...].T.astype(LOW)
    dtok_ref[...] = (
        mm(d_ref[:, :width], wq[...], 1, 1)
        + mm(d_ref[:, width : 2 * width], wk[...], 1, 1)
        + mm(d_ref[:, 2 * width :], wv[...], 1, 1)
    ).astype(dtok_ref.dtype)


def attend_back(info, saved, do, wq, wk, wv, prev, count, slot):
    q, k, v, lse = saved
    model, width = wq.shape
    full = lambda a: pl.BlockSpec(a.shape, lambda i, s: (0, 0))
    return pl.pallas_call(
        attend_back_kernel,
        grid_spec=pltpu.PrefetchScalarGridSpec(
            num_scalar_prefetch=1,
            grid=(1,),
            in_specs=[full(a) for a in (q, k, v, lse, do, wq, wk, wv)] + [pl.BlockSpec(memory_space=pl.ANY)],
            out_specs=[
                pl.BlockSpec((slot, 3 * width), lambda i, s: (s[0], 0)),
                pl.BlockSpec((slot, model), lambda i, s: (0, 0)),
            ],
            scratch_shapes=[pltpu.VMEM((width, slot), F32)],
        ),
        out_shape=[
            jax.ShapeDtypeStruct((count, 3 * width), LOW),
            jax.ShapeDtypeStruct((slot, model), LOW),
        ],
        input_output_aliases={9: 0},
        cost_estimate=pl.CostEstimate(flops=8 * 10**9, transcendentals=2 * 10**6, bytes_accessed=6 * 10**6),
        name="attend_back",
    )(info, q, k, v, lse, do, wq, wk, wv, prev)


def swap(x, axis, flip):
    size = lax.axis_size(axis)
    return lax.ppermute(x, axis, [(i, i ^ flip) for i in range(size)])


def rows_at(x, start, size):
    return lax.dynamic_slice_in_dim(x, start, size, 0)


def scatter_stage(x, place, low, bits):
    parts = 1 << bits
    share = x.shape[0] // parts
    own = (place >> low) & (parts - 1)
    total = rows_at(x, own * share, share).astype(F32)
    for d in range(1, parts):
        total = total + swap(rows_at(x, (own ^ d) * share, share), "dp", d << low).astype(F32)
    return total.astype(LOW)


def gather_stage(x, place, low, bits):
    parts = 1 << bits
    share = x.shape[0]
    own = (place >> low) & (parts - 1)
    out = jnp.zeros((share * parts,) + x.shape[1:], x.dtype)
    out = lax.dynamic_update_slice_in_dim(out, x, own * share, 0)
    for d in range(1, parts):
        out = lax.dynamic_update_slice_in_dim(out, swap(x, "dp", d << low), (own ^ d) * share, 0)
    return out


def stages(first, size, most):
    out = []
    while (1 << first) < size:
        bits = 0
        while bits < most and (1 << (first + bits)) < size:
            bits += 1
        out.append((first, bits))
        first += bits
    return out


def sum_over(x, place, plan):
    for low, bits in plan:
        x = scatter_stage(x, place, low, bits)
    return x


def gather_over(x, place, plan):
    for low, bits in reversed(plan):
        x = gather_stage(x, place, low, bits)
    return x


def all_sum(x, place, plan):
    for low, bits in plan:
        total = x
        for d in range(1, 1 << bits):
            total = total + swap(x, "dp", d << low)
        x = total
    return x


def norm(values):
    center = values - jnp.mean(values, axis=-1, keepdims=True)
    root = lax.rsqrt(jnp.mean(center * center, axis=-1, keepdims=True) + 1e-05)
    return center * root, root


def norm_back(grad, n, root):
    return root * (grad - jnp.mean(grad, axis=-1, keepdims=True) - n * jnp.mean(grad * n, axis=-1, keepdims=True))


def gate(u):
    c = 0.7978845608028654
    square = u * u
    t = jnp.tanh(u * (c + (c * 0.044715) * square))
    half = 0.5 + 0.5 * t
    active = u * half
    slope = half + active * (1.0 - t) * (c + (3 * c * 0.044715) * square)
    return active, slope


def shards(
    tokens,
    window_length,
    query_weight,
    query_bias,
    key_weight,
    value_weight,
    value_bias,
    output_weight,
    output_bias,
    first_gain,
    first_shift,
    inner_weight,
    inner_bias,
    outer_weight,
    outer_bias,
    second_gain,
    second_shift,
    cotangent,
):
    count, model = tokens.shape
    windows = window_length.shape[0]
    slot = count // windows
    half = slot // 2
    share = count // 2
    width = query_weight.shape[1]
    m = lax.axis_index("mp")
    place = lax.axis_index("dp")
    dps = lax.axis_size("dp")
    core = place & 1
    cross = lambda x: swap(x, "mp", 1)
    beside = lambda x: swap(x, "dp", 1)
    f32 = lambda x: x.astype(F32)

    wo_half = output_weight.shape[0] // 2
    ff = inner_weight.shape[1] // 2
    wo_part = cross(rows_at(output_weight, core * wo_half, wo_half))
    wo_peer = gather_stage(wo_part, place, 0, 1)
    wi = [lax.dynamic_slice_in_dim(inner_weight, c * ff, ff, 1) for c in (core, 1 - core)]
    wu = [rows_at(outer_weight, c * ff, ff) for c in (core, 1 - core)]
    bi_peer = cross(inner_bias)
    bi = [rows_at(b, c * ff, ff) for b in (inner_bias, bi_peer) for c in (core, 1 - core)]
    wi.append(cross(wi[0]))
    wu.append(cross(wu[0]))
    wi.append(beside(wi[2]))
    wu.append(beside(wu[2]))

    order = [jnp.where(m == 0, 2 - i, i) for i in range(3)]
    infos = [jnp.stack([w, window_length[w]]) for w in order]
    bq = f32(query_bias)[None]
    bv = f32(value_bias)[None]
    done = [attend(info, tokens, query_weight, key_weight, value_weight, bq, bv, slot) for info in infos]
    mixed = [d[3] for d in done]
    got_win = cross(mixed[0])
    got_half = cross(rows_at(mixed[1], (1 - m) * half, half))
    mix_own = rows_at(jnp.concatenate([mixed[2], mixed[1], mixed[2]]), m * share, share)
    mix_peer = rows_at(jnp.concatenate([got_win, got_half, got_win]), m * slot, share)

    tok_own = f32(rows_at(tokens, m * share, share))
    first_in = tok_own + mm(mix_own, output_weight) + mm(mix_peer, wo_peer) + f32(output_bias)
    n1, root1 = norm(first_in)
    normed = n1 * f32(first_gain) + f32(first_shift)
    low_normed = normed.astype(LOW)
    actives = []
    slopes = []
    second_in = normed + f32(outer_bias)
    for b in range(4):
        a, s = gate(mm(low_normed, wi[b]) + f32(bi[b]))
        actives.append(a.astype(LOW))
        slopes.append(s.astype(LOW))
        second_in = second_in + mm(actives[b], wu[b])
    n2, root2 = norm(second_in)
    layer_out = (n2 * f32(second_gain) + f32(second_shift)).astype(LOW)
    cot = f32(cotangent)
    dsecond = norm_back(cot * f32(second_gain), n2, root2)
    db2 = dsecond.astype(LOW)
    second_ggrad = jnp.sum(cot * n2, axis=0)
    second_sgrad = jnp.sum(cot, axis=0)
    outer_bgrad = jnp.sum(f32(db2), axis=0)
    dnormed = dsecond
    dwi = []
    dwu = []
    dbi = []
    for b in range(4):
        dwu.append(mm(actives[b], db2, 0, 0).astype(LOW))
        dinner = (mm(db2, wu[b], 1, 1) * f32(slopes[b])).astype(LOW)
        dbi.append(jnp.sum(f32(dinner), axis=0))
        dwi.append(mm(low_normed, dinner, 0, 0).astype(LOW))
        dnormed = dnormed + mm(dinner, wi[b], 1, 1)
    first_ggrad = jnp.sum(dnormed * n1, axis=0)
    first_sgrad = jnp.sum(dnormed, axis=0)
    dfirst = norm_back(dnormed * f32(first_gain), n1, root1)
    db1 = dfirst.astype(LOW)
    output_bgrad = jnp.sum(f32(db1), axis=0)
    dmix_own = mm(db1, output_weight, 1, 1).astype(LOW)
    dmix_peer = mm(db1, wo_peer, 1, 1).astype(LOW)
    dwo_own = mm(mix_own, db1, 0, 0).astype(LOW)
    dwo_peer = mm(mix_peer, db1, 0, 0).astype(LOW)

    got_dwin = cross(rows_at(dmix_peer, m * half, slot))
    got_dhalf = cross(rows_at(dmix_peer, (1 - m) * slot, half))
    own_dwin = rows_at(dmix_own, m * half, slot)
    own_dhalf = rows_at(dmix_own, (1 - m) * slot, half)
    dmid = rows_at(jnp.concatenate([own_dhalf, got_dhalf, own_dhalf]), m * half, slot)
    grads = jnp.zeros((count, 3 * width), LOW)
    dtok = []
    for role, do in ((2, own_dwin), (1, dmid), (0, got_dwin)):
        saved = (*done[role][:3], done[role][4])
        grads, dt = attend_back(
            infos[role], saved, do, query_weight, key_weight, value_weight, grads, count, slot
        )
        dtok.append(dt)
    got_thalf = cross(rows_at(dtok[1], (1 - m) * half, half))
    got_twin = cross(dtok[2])
    dtok_own = rows_at(jnp.concatenate([dtok[0], dtok[1], dtok[0]]), m * share, share)
    dtok_peer = rows_at(jnp.concatenate([got_twin, got_thalf, got_twin]), m * slot, share)
    tokens_grad = dfirst + f32(dtok_own) + f32(dtok_peer)

    plan = [(1, 1)] + stages(2, dps, 2)
    if dps <= 2:
        plan = []

    def reduce_blocks(own_same, own_other, peer_same, peer_other):
        mine = (f32(own_same) + f32(beside(own_other))).astype(LOW)
        other = (f32(peer_same) + f32(beside(peer_other))).astype(LOW)
        total = (f32(mine) + f32(cross(other))).astype(LOW)
        return gather_over(sum_over(total, place, plan), place, plan)

    red_u = reduce_blocks(*dwu)
    red_i = reduce_blocks(*dwi)
    outer_wgrad = f32(gather_stage(red_u, place, 0, 1))
    red_i2 = beside(red_i)
    inner_wgrad = f32(
        jnp.where(core == 0, jnp.concatenate([red_i, red_i2], 1), jnp.concatenate([red_i2, red_i], 1))
    )
    direct = stages(1, dps, 3)
    red_o = reduce_o = None
    same = lambda x: rows_at(x, core * wo_half, wo_half)
    other = lambda x: rows_at(x, (1 - core) * wo_half, wo_half)
    own = (f32(same(dwo_own)) + f32(beside(other(dwo_own)))).astype(LOW)
    peer = (f32(same(dwo_peer)) + f32(beside(other(dwo_peer)))).astype(LOW)
    red_o = (f32(own) + f32(cross(peer))).astype(LOW)
    red_o = gather_over(sum_over(red_o, place, direct), place, direct)
    output_wgrad = f32(gather_stage(red_o, place, 0, 1))

    dqkv = mm(tokens, grads, 0, 0).astype(LOW)
    bias_q = jnp.sum(f32(grads[:, :width]), axis=0)
    bias_v = jnp.sum(f32(grads[:, 2 * width :]), axis=0)
    path = [(0, 1)] + direct
    dqkv = f32(gather_over(sum_over(dqkv, place, path), place, path))

    both = jnp.stack([output_bgrad, first_ggrad, first_sgrad, outer_bgrad, second_ggrad, second_sgrad])
    both = both + cross(both)
    dbi_own = lax.dynamic_update_slice_in_dim(
        lax.dynamic_update_slice_in_dim(jnp.zeros((2 * ff,), F32), dbi[0], core * ff, 0), dbi[1], (1 - core) * ff, 0
    )
    dbi_peer = lax.dynamic_update_slice_in_dim(
        lax.dynamic_update_slice_in_dim(jnp.zeros((2 * ff,), F32), dbi[2], core * ff, 0), dbi[3], (1 - core) * ff, 0
    )
    dbi_own = dbi_own + cross(dbi_peer)
    small = jnp.concatenate([both.reshape(-1), dbi_own, bias_q, bias_v])
    small = all_sum(small.reshape(-1, 128), place, path).reshape(-1)
    six = small[: 6 * model].reshape(6, model)
    at = 6 * model
    return (
        layer_out,
        tokens_grad,
        dqkv[:, :width],
        small[at + 2 * ff : at + 2 * ff + width],
        dqkv[:, width : 2 * width],
        dqkv[:, 2 * width :],
        small[at + 2 * ff + width :],
        output_wgrad,
        six[0],
        six[1],
        six[2],
        inner_wgrad,
        small[at : at + 2 * ff],
        outer_wgrad,
        six[3],
        six[4],
        six[5],
    )


def solution(mesh):
    in_specs = (
        P("dp", None),
        P("dp"),
        P(None, "mp"),
        P("mp"),
        P(None, "mp"),
        P(None, "mp"),
        P("mp"),
        P("mp", None),
        P(),
        P(),
        P(),
        P(None, "mp"),
        P("mp"),
        P("mp", None),
        P(),
        P(),
        P(),
        P(("dp", "mp"), None),
    )
    out_specs = (
        P(("dp", "mp"), None),
        P(("dp", "mp"), None),
        P(None, "mp"),
        P("mp"),
        P(None, "mp"),
        P(None, "mp"),
        P("mp"),
        P("mp", None),
        P(),
        P(),
        P(),
        P(None, "mp"),
        P("mp"),
        P("mp", None),
        P(),
        P(),
        P(),
    )
    return jax.shard_map(shards, mesh=mesh, in_specs=in_specs, out_specs=out_specs, check_vma=False)
```

```python
import jax
import jax.numpy as jnp
from jax import lax
from jax.experimental import pallas as pl
from jax.experimental.pallas import tpu as pltpu
from jax.sharding import PartitionSpec as P

HEAD = 64
PAIR = 128
LOW = jnp.bfloat16
F32 = jnp.float32


def mm(a, b, ca=1, cb=0):
    return lax.dot_general(a, b, (((ca,), (cb,)), ((), ())), preferred_element_type=F32)


def allowed_mask(length, slot):
    rows = lax.broadcasted_iota(jnp.int32, (slot, slot), 0)
    cols = lax.broadcasted_iota(jnp.int32, (slot, slot), 1)
    return (rows ^ cols) < length


def attend_kernel(info, tok, wq, wk, wv, bq, bv, q_ref, k_ref, v_ref, mix_ref, lse_ref, mixt):
    tokens = tok[...]
    q_ref[...] = (mm(tokens, wq[...]) + bq[...]).astype(LOW)
    k_ref[...] = mm(tokens, wk[...]).astype(LOW)
    v_ref[...] = (mm(tokens, wv[...]) + bv[...]).astype(LOW)
    slot, width = q_ref.shape
    length = info[1]
    scale = HEAD ** (-0.5)

    def heads(masked):
        allowed = allowed_mask(length, slot) if masked else None
        @pl.loop(0, width // PAIR)
        def _(pair):
            lanes = pl.ds(pl.multiple_of(pair * PAIR, PAIR), PAIR)
            q2 = q_ref[:, lanes] * LOW(scale)
            k2 = k_ref[:, lanes]
            v2 = v_ref[:, lanes]
            for j in range(PAIR // HEAD):
                cut = slice(j * HEAD, (j + 1) * HEAD)
                scores = mm(k2[:, cut], q2[:, cut], 1, 1)
                if masked:
                    scores = jnp.where(allowed, scores, -1e30)
                top = jnp.max(scores, axis=0, keepdims=True)
                weights = jnp.exp(scores - top)
                total = jnp.sum(weights, axis=0, keepdims=True)
                lse_ref[pl.ds(pair * (PAIR // HEAD) + j, 1), :] = top + jnp.log(total)
                part = mm(v2[:, cut], weights.astype(LOW), 0, 0)
                mixt[pl.ds(pl.multiple_of(pair * PAIR + j * HEAD, HEAD), HEAD), :] = part / total

    @pl.when(length < slot)
    def _():
        heads(True)

    @pl.when(length >= slot)
    def _():
        heads(False)

    mix_ref[...] = mixt[...].T.astype(LOW)


def attend(info, tokens, wq, wk, wv, bq, bv, slot):
    count, model = tokens.shape
    width = wq.shape[1]
    rows = (width // HEAD + 7) // 8 * 8
    full = lambda a: pl.BlockSpec(a.shape, lambda i, s: (0, 0))
    piece = lambda: pl.BlockSpec((slot, width), lambda i, s: (0, 0))
    return pl.pallas_call(
        attend_kernel,
        grid_spec=pltpu.PrefetchScalarGridSpec(
            num_scalar_prefetch=1,
            grid=(1,),
            in_specs=[pl.BlockSpec((slot, model), lambda i, s: (s[0], 0))]
            + [full(a) for a in (wq, wk, wv, bq, bv)],
            out_specs=[piece(), piece(), piece(), piece(), pl.BlockSpec((rows, slot), lambda i, s: (0, 0))],
            scratch_shapes=[pltpu.VMEM((width, slot), F32)],
        ),
        out_shape=[jax.ShapeDtypeStruct((slot, width), LOW)] * 4
        + [jax.ShapeDtypeStruct((rows, slot), F32)],
        cost_estimate=pl.CostEstimate(flops=4 * 10**9, transcendentals=2 * 10**6, bytes_accessed=4 * 10**6),
        name="attend",
    )(info, tokens, wq, wk, wv, bq, bv)


def attend_back_kernel(info, q_ref, k_ref, v_ref, lse_ref, do_ref, wq, wk, wv, prev, d_ref, dtok_ref, dqt):
    slot, width = q_ref.shape
    length = info[1]
    scale = HEAD ** (-0.5)

    def heads(masked):
        allowed = allowed_mask(length, slot) if masked else None
        @pl.loop(0, width // PAIR)
        def _(pair):
            base = pl.multiple_of(pair * PAIR, PAIR)
            lanes = pl.ds(base, PAIR)
            q2 = q_ref[:, lanes] * LOW(scale)
            k2 = k_ref[:, lanes]
            v2 = v_ref[:, lanes]
            do2 = do_ref[:, lanes]
            dks = []
            dvs = []
            for j in range(PAIR // HEAD):
                cut = slice(j * HEAD, (j + 1) * HEAD)
                q, k, v, do = q2[:, cut], k2[:, cut], v2[:, cut], do2[:, cut]
                scores = mm(k, q, 1, 1)
                if masked:
                    scores = jnp.where(allowed, scores, -1e30)
                probs = jnp.exp(scores - lse_ref[pl.ds(pair * (PAIR // HEAD) + j, 1), :])
                dprobs = mm(v, do, 1, 1)
                inner = jnp.sum(probs * dprobs, axis=0, keepdims=True)
                ds = (probs * (dprobs - inner)).astype(LOW)
                dvs.append(mm(probs.astype(LOW), do))
                dks.append(mm(ds, q))
                dqt[pl.ds(pl.multiple_of(base + j * HEAD, HEAD), HEAD), :] = mm(k, ds, 0, 0) * scale
            d_ref[:, pl.ds(pl.multiple_of(2 * width + base, PAIR), PAIR)] = jnp.concatenate(dvs, 1).astype(LOW)
            d_ref[:, pl.ds(pl.multiple_of(width + base, PAIR), PAIR)] = jnp.concatenate(dks, 1).astype(LOW)

    @pl.when(length < slot)
    def _():
        heads(True)

    @pl.when(length >= slot)
    def _():
        heads(False)

    d_ref[:, :width] = dqt[...].T.astype(LOW)
    dtok_ref[...] = (
        mm(d_ref[:, :width], wq[...], 1, 1)
        + mm(d_ref[:, width : 2 * width], wk[...], 1, 1)
        + mm(d_ref[:, 2 * width :], wv[...], 1, 1)
    ).astype(dtok_ref.dtype)


def attend_back(info, saved, do, wq, wk, wv, prev, count, slot):
    q, k, v, lse = saved
    model, width = wq.shape
    full = lambda a: pl.BlockSpec(a.shape, lambda i, s: (0, 0))
    return pl.pallas_call(
        attend_back_kernel,
        grid_spec=pltpu.PrefetchScalarGridSpec(
            num_scalar_prefetch=1,
            grid=(1,),
            in_specs=[full(a) for a in (q, k, v, lse, do, wq, wk, wv)] + [pl.BlockSpec(memory_space=pl.ANY)],
            out_specs=[
                pl.BlockSpec((slot, 3 * width), lambda i, s: (s[0], 0)),
                pl.BlockSpec((slot, model), lambda i, s: (0, 0)),
            ],
            scratch_shapes=[pltpu.VMEM((width, slot), F32)],
        ),
        out_shape=[
            jax.ShapeDtypeStruct((count, 3 * width), LOW),
            jax.ShapeDtypeStruct((slot, model), LOW),
        ],
        input_output_aliases={9: 0},
        cost_estimate=pl.CostEstimate(flops=8 * 10**9, transcendentals=2 * 10**6, bytes_accessed=6 * 10**6),
        name="attend_back",
    )(info, q, k, v, lse, do, wq, wk, wv, prev)


def swap(x, axis, flip):
    size = lax.axis_size(axis)
    return lax.ppermute(x, axis, [(i, i ^ flip) for i in range(size)])


def rows_at(x, start, size):
    return lax.dynamic_slice_in_dim(x, start, size, 0)


def scatter_stage(x, place, low, bits):
    parts = 1 << bits
    share = x.shape[0] // parts
    own = (place >> low) & (parts - 1)
    total = rows_at(x, own * share, share).astype(F32)
    for d in range(1, parts):
        total = total + swap(rows_at(x, (own ^ d) * share, share), "dp", d << low).astype(F32)
    return total.astype(LOW)


def gather_stage(x, place, low, bits):
    parts = 1 << bits
    share = x.shape[0]
    own = (place >> low) & (parts - 1)
    if parts == 2:
        y = swap(x, "dp", 1 << low)
        return jnp.where(own == 0, jnp.concatenate([x, y]), jnp.concatenate([y, x]))
    out = jnp.zeros((share * parts,) + x.shape[1:], x.dtype)
    out = lax.dynamic_update_slice_in_dim(out, x, own * share, 0)
    for d in range(1, parts):
        out = lax.dynamic_update_slice_in_dim(out, swap(x, "dp", d << low), (own ^ d) * share, 0)
    return out


def stages(first, size, most):
    out = []
    while (1 << first) < size:
        bits = 0
        while bits < most and (1 << (first + bits)) < size:
            bits += 1
        out.append((first, bits))
        first += bits
    return out


def sum_over(x, place, plan):
    for low, bits in plan:
        x = scatter_stage(x, place, low, bits)
    return x


def gather_over(x, place, plan):
    for low, bits in reversed(plan):
        x = gather_stage(x, place, low, bits)
    return x


def all_sum(x, place, plan):
    for low, bits in plan:
        total = x
        for d in range(1, 1 << bits):
            total = total + swap(x, "dp", d << low)
        x = total
    return x


def norm(values):
    center = values - jnp.mean(values, axis=-1, keepdims=True)
    root = lax.rsqrt(jnp.mean(center * center, axis=-1, keepdims=True) + 1e-05)
    return center * root, root


def norm_back(grad, n, root):
    return root * (grad - jnp.mean(grad, axis=-1, keepdims=True) - n * jnp.mean(grad * n, axis=-1, keepdims=True))


def gate(u):
    c = 0.7978845608028654
    square = u * u
    t = jnp.tanh(u * (c + (c * 0.044715) * square))
    half = 0.5 + 0.5 * t
    active = u * half
    slope = half + active * (1.0 - t) * (c + (3 * c * 0.044715) * square)
    return active, slope


def shards(
    tokens,
    window_length,
    query_weight,
    query_bias,
    key_weight,
    value_weight,
    value_bias,
    output_weight,
    output_bias,
    first_gain,
    first_shift,
    inner_weight,
    inner_bias,
    outer_weight,
    outer_bias,
    second_gain,
    second_shift,
    cotangent,
):
    count, model = tokens.shape
    windows = window_length.shape[0]
    slot = count // windows
    half = slot // 2
    share = count // 2
    width = query_weight.shape[1]
    m = lax.axis_index("mp")
    place = lax.axis_index("dp")
    dps = lax.axis_size("dp")
    core = place & 1
    cross = lambda x: swap(x, "mp", 1)
    beside = lambda x: swap(x, "dp", 1)
    f32 = lambda x: x.astype(F32)

    wo_half = output_weight.shape[0] // 2
    ff = inner_weight.shape[1] // 2
    wo_part = cross(rows_at(output_weight, core * wo_half, wo_half))
    wo_peer = gather_stage(wo_part, place, 0, 1)
    wi = [lax.dynamic_slice_in_dim(inner_weight, c * ff, ff, 1) for c in (core, 1 - core)]
    wu = [rows_at(outer_weight, c * ff, ff) for c in (core, 1 - core)]
    bi_peer = cross(inner_bias)
    bi = [rows_at(b, c * ff, ff) for b in (inner_bias, bi_peer) for c in (core, 1 - core)]
    hop = 2 if dps > 4 else 1

    def fetch(same, low):
        if dps <= 2:
            return cross(same)
        return gather_stage(cross(rows_at(same, ((place >> low) & 1) * (same.shape[0] // 2), same.shape[0] // 2)), place, low, 1)

    wi.append(fetch(wi[0], 1))
    wu.append(fetch(wu[0], hop))
    wi.append(beside(wi[2]))
    wu.append(beside(wu[2]))

    order = [jnp.where(m == 0, 2 - i, i) for i in range(3)]
    infos = [jnp.stack([w, window_length[w]]) for w in order]
    bq = f32(query_bias)[None]
    bv = f32(value_bias)[None]
    done = [attend(info, tokens, query_weight, key_weight, value_weight, bq, bv, slot) for info in infos]
    mixed = [d[3] for d in done]
    got_win = cross(mixed[0])
    got_half = cross(rows_at(mixed[1], (1 - m) * half, half))
    mix_own = rows_at(jnp.concatenate([mixed[2], mixed[1], mixed[2]]), m * share, share)
    mix_peer = rows_at(jnp.concatenate([got_win, got_half, got_win]), m * slot, share)

    tok_own = f32(rows_at(tokens, m * share, share))
    first_in = tok_own + mm(mix_own, output_weight) + mm(mix_peer, wo_peer) + f32(output_bias)
    n1, root1 = norm(first_in)
    normed = n1 * f32(first_gain) + f32(first_shift)
    low_normed = normed.astype(LOW)
    actives = []
    slopes = []
    second_in = normed + f32(outer_bias)
    for b in range(4):
        a, s = gate(mm(low_normed, wi[b]) + f32(bi[b]))
        actives.append(a.astype(LOW))
        slopes.append(s.astype(LOW))
        second_in = second_in + mm(actives[b], wu[b])
    n2, root2 = norm(second_in)
    layer_out = (n2 * f32(second_gain) + f32(second_shift)).astype(LOW)
    cot = f32(cotangent)
    dsecond = norm_back(cot * f32(second_gain), n2, root2)
    db2 = dsecond.astype(LOW)
    second_ggrad = jnp.sum(cot * n2, axis=0)
    second_sgrad = jnp.sum(cot, axis=0)
    outer_bgrad = jnp.sum(f32(db2), axis=0)
    dnormed = dsecond
    dwi = []
    dwu = []
    dbi = []
    for b in range(4):
        dwu.append(mm(actives[b], db2, 0, 0).astype(LOW))
        dinner = (mm(db2, wu[b], 1, 1) * f32(slopes[b])).astype(LOW)
        dbi.append(jnp.sum(f32(dinner), axis=0))
        dwi.append(mm(low_normed, dinner, 0, 0).astype(LOW))
        dnormed = dnormed + mm(dinner, wi[b], 1, 1)
    first_ggrad = jnp.sum(dnormed * n1, axis=0)
    first_sgrad = jnp.sum(dnormed, axis=0)
    dfirst = norm_back(dnormed * f32(first_gain), n1, root1)
    db1 = dfirst.astype(LOW)
    output_bgrad = jnp.sum(f32(db1), axis=0)
    dmix_own = mm(db1, output_weight, 1, 1).astype(LOW)
    dmix_peer = mm(db1, wo_peer, 1, 1).astype(LOW)
    dwo_own = mm(mix_own, db1, 0, 0).astype(LOW)
    dwo_peer = mm(mix_peer, db1, 0, 0).astype(LOW)

    plan = stages(1, 2, 1) if dps <= 2 else stages(1, dps, 1)
    rest = plan[1:]
    direct = stages(1, 4, 1) + stages(2, dps, 2) if dps > 4 else stages(1, dps, 1)
    u_same = (f32(dwu[0]) + f32(beside(dwu[1]))).astype(LOW)
    u_peer = (f32(dwu[2]) + f32(beside(dwu[3]))).astype(LOW)
    i_both = jnp.concatenate([dwi[0], dwi[2]], 1)
    i_both = (f32(i_both) + f32(beside(jnp.concatenate([dwi[1], dwi[3]], 1)))).astype(LOW)
    u_got = cross(u_peer)
    dmix_own, u_same, i_both = lax.optimization_barrier((dmix_own, u_same, i_both))

    same = lambda x: rows_at(x, core * wo_half, wo_half)
    other = lambda x: rows_at(x, (1 - core) * wo_half, wo_half)
    join = lambda a, b: jnp.where(core == 0, jnp.concatenate([a, b]), jnp.concatenate([b, a]))
    six = jnp.stack([output_bgrad, first_ggrad, first_sgrad, outer_bgrad, second_ggrad, second_sgrad])
    dbi_own = join(dbi[0], dbi[1])
    dbi_own = dbi_own + cross(join(dbi[2], dbi[3]))

    got_dwin = cross(rows_at(dmix_peer, m * half, slot))
    got_dhalf = cross(rows_at(dmix_peer, (1 - m) * slot, half))
    own_dwin = rows_at(dmix_own, m * half, slot)
    own_dhalf = rows_at(dmix_own, (1 - m) * slot, half)
    dmid = rows_at(jnp.concatenate([own_dhalf, got_dhalf, own_dhalf]), m * half, slot)
    grads = jnp.zeros((count, 3 * width), LOW)
    dtok = []
    small_rows = 64
    for role, do in ((2, own_dwin), (1, dmid), (0, got_dwin)):
        if role == 1:
            o_own = (f32(same(dwo_own)) + f32(beside(other(dwo_own)))).astype(LOW)
            o_peer = (f32(same(dwo_peer)) + f32(beside(other(dwo_peer)))).astype(LOW)
            grads, o_own, o_peer = lax.optimization_barrier((grads, o_own, o_peer))
            o_got = cross(o_peer)
            six = six + cross(six)
            six = six + beside(six)
        if role == 0:
            u_sum = (f32(u_same) + f32(u_got)).astype(LOW)
            o_sum = (f32(o_own) + f32(o_got)).astype(LOW)
            tail = jnp.zeros((small_rows - six.shape[0], model), LOW)
            u_all = jnp.concatenate([u_sum, o_sum, six.astype(LOW), tail])
            i_sum = scatter_stage(i_both, place, *plan[0]) if plan else i_both
            grads, u_all, i_sum = lax.optimization_barrier((grads, u_all, i_sum))
        saved = (*done[role][:3], done[role][4])
        grads, dt = attend_back(
            infos[role], saved, do, query_weight, key_weight, value_weight, grads, count, slot
        )
        dtok.append(dt)
    got_thalf = cross(rows_at(dtok[1], (1 - m) * half, half))
    got_twin = cross(dtok[2])
    dtok_own = rows_at(jnp.concatenate([dtok[0], dtok[1], dtok[0]]), m * share, share)
    dtok_peer = rows_at(jnp.concatenate([got_twin, got_thalf, got_twin]), m * slot, share)
    tokens_grad = dfirst + f32(dtok_own) + f32(dtok_peer)

    dqkv = mm(tokens, grads, 0, 0).astype(LOW)
    bias_q = jnp.sum(f32(grads[:, :width]), axis=0)
    bias_v = jnp.sum(f32(grads[:, 2 * width :]), axis=0)
    path = [(0, 1)] + direct
    dqkv = f32(gather_over(sum_over(dqkv, place, path), place, path))

    bias = jnp.concatenate([dbi_own, bias_q, bias_v])
    bias = all_sum(bias.reshape(-1, 128), place, path).reshape(-1)

    u_all = gather_over(sum_over(u_all, place, plan), place, plan)
    i_sum = sum_over(i_sum, place, rest)
    i_sum = (f32(i_sum[:, :ff]) + f32(cross(i_sum[:, ff:]))).astype(LOW)
    i_sum = gather_over(i_sum, place, plan)
    u_red = u_all[:ff]
    o_red = u_all[ff : ff + wo_half]
    six = f32(u_all[ff + wo_half : ff + wo_half + 6])
    u_beside = beside(u_all)
    i_beside = beside(i_sum)
    outer_wgrad = f32(join(u_red, u_beside[:ff]))
    output_wgrad = f32(join(o_red, u_beside[ff : ff + wo_half]))
    inner_wgrad = f32(
        jnp.where(core == 0, jnp.concatenate([i_sum, i_beside], 1), jnp.concatenate([i_beside, i_sum], 1))
    )
    return (
        layer_out,
        tokens_grad,
        dqkv[:, :width],
        bias[2 * ff : 2 * ff + width],
        dqkv[:, width : 2 * width],
        dqkv[:, 2 * width :],
        bias[2 * ff + width :],
        output_wgrad,
        six[0],
        six[1],
        six[2],
        inner_wgrad,
        bias[: 2 * ff],
        outer_wgrad,
        six[3],
        six[4],
        six[5],
    )


def solution(mesh):
    in_specs = (
        P("dp", None),
        P("dp"),
        P(None, "mp"),
        P("mp"),
        P(None, "mp"),
        P(None, "mp"),
        P("mp"),
        P("mp", None),
        P(),
        P(),
        P(),
        P(None, "mp"),
        P("mp"),
        P("mp", None),
        P(),
        P(),
        P(),
        P(("dp", "mp"), None),
    )
    out_specs = (
        P(("dp", "mp"), None),
        P(("dp", "mp"), None),
        P(None, "mp"),
        P("mp"),
        P(None, "mp"),
        P(None, "mp"),
        P("mp"),
        P("mp", None),
        P(),
        P(),
        P(),
        P(None, "mp"),
        P("mp"),
        P("mp", None),
        P(),
        P(),
        P(),
    )
    return jax.shard_map(shards, mesh=mesh, in_specs=in_specs, out_specs=out_specs, check_vma=False)
```

```python
import jax
import jax.numpy as jnp
from jax import lax
from jax.experimental import pallas as pl
from jax.experimental.pallas import tpu as pltpu
from jax.sharding import PartitionSpec as P

HEAD = 64
PAIR = 128
LOW = jnp.bfloat16
F32 = jnp.float32


def mm(a, b, ca=1, cb=0):
    return lax.dot_general(a, b, (((ca,), (cb,)), ((), ())), preferred_element_type=F32)


def allowed_mask(length, slot):
    rows = lax.broadcasted_iota(jnp.int32, (slot, slot), 0)
    cols = lax.broadcasted_iota(jnp.int32, (slot, slot), 1)
    return (rows ^ cols) < length


def attend_kernel(info, tok, wq, wk, wv, bq, bv, q_ref, k_ref, v_ref, mix_ref, lse_ref, mixt):
    tokens = tok[...]
    q_ref[...] = (mm(tokens, wq[...]) + bq[...]).astype(LOW)
    k_ref[...] = mm(tokens, wk[...]).astype(LOW)
    v_ref[...] = (mm(tokens, wv[...]) + bv[...]).astype(LOW)
    slot, width = q_ref.shape
    length = info[1]
    scale = HEAD ** (-0.5)

    def heads(masked):
        allowed = allowed_mask(length, slot) if masked else None
        @pl.loop(0, width // PAIR)
        def _(pair):
            lanes = pl.ds(pl.multiple_of(pair * PAIR, PAIR), PAIR)
            q2 = q_ref[:, lanes] * LOW(scale)
            k2 = k_ref[:, lanes]
            v2 = v_ref[:, lanes]
            for j in range(PAIR // HEAD):
                cut = slice(j * HEAD, (j + 1) * HEAD)
                scores = mm(k2[:, cut], q2[:, cut], 1, 1)
                if masked:
                    scores = jnp.where(allowed, scores, -1e30)
                top = jnp.max(scores, axis=0, keepdims=True)
                weights = jnp.exp(scores - top)
                total = jnp.sum(weights, axis=0, keepdims=True)
                lse_ref[pl.ds(pair * (PAIR // HEAD) + j, 1), :] = top + jnp.log(total)
                part = mm(v2[:, cut], weights.astype(LOW), 0, 0)
                mixt[pl.ds(pl.multiple_of(pair * PAIR + j * HEAD, HEAD), HEAD), :] = part / total

    @pl.when(length < slot)
    def _():
        heads(True)

    @pl.when(length >= slot)
    def _():
        heads(False)

    mix_ref[...] = mixt[...].T.astype(LOW)


def attend(info, tokens, wq, wk, wv, bq, bv, slot):
    count, model = tokens.shape
    width = wq.shape[1]
    rows = (width // HEAD + 7) // 8 * 8
    full = lambda a: pl.BlockSpec(a.shape, lambda i, s: (0, 0))
    piece = lambda: pl.BlockSpec((slot, width), lambda i, s: (0, 0))
    return pl.pallas_call(
        attend_kernel,
        grid_spec=pltpu.PrefetchScalarGridSpec(
            num_scalar_prefetch=1,
            grid=(1,),
            in_specs=[pl.BlockSpec((slot, model), lambda i, s: (s[0], 0))]
            + [full(a) for a in (wq, wk, wv, bq, bv)],
            out_specs=[piece(), piece(), piece(), piece(), pl.BlockSpec((rows, slot), lambda i, s: (0, 0))],
            scratch_shapes=[pltpu.VMEM((width, slot), F32)],
        ),
        out_shape=[jax.ShapeDtypeStruct((slot, width), LOW)] * 4
        + [jax.ShapeDtypeStruct((rows, slot), F32)],
        cost_estimate=pl.CostEstimate(flops=4 * 10**9, transcendentals=2 * 10**6, bytes_accessed=4 * 10**6),
        name="attend",
    )(info, tokens, wq, wk, wv, bq, bv)


def attend_back_kernel(info, q_ref, k_ref, v_ref, lse_ref, do_ref, wq, wk, wv, prev, d_ref, dtok_ref, dqt):
    slot, width = q_ref.shape
    length = info[1]
    scale = HEAD ** (-0.5)

    def heads(masked):
        allowed = allowed_mask(length, slot) if masked else None
        @pl.loop(0, width // PAIR)
        def _(pair):
            base = pl.multiple_of(pair * PAIR, PAIR)
            lanes = pl.ds(base, PAIR)
            q2 = q_ref[:, lanes] * LOW(scale)
            k2 = k_ref[:, lanes]
            v2 = v_ref[:, lanes]
            do2 = do_ref[:, lanes]
            dks = []
            dvs = []
            for j in range(PAIR // HEAD):
                cut = slice(j * HEAD, (j + 1) * HEAD)
                q, k, v, do = q2[:, cut], k2[:, cut], v2[:, cut], do2[:, cut]
                scores = mm(k, q, 1, 1)
                if masked:
                    scores = jnp.where(allowed, scores, -1e30)
                probs = jnp.exp(scores - lse_ref[pl.ds(pair * (PAIR // HEAD) + j, 1), :])
                dprobs = mm(v, do, 1, 1)
                inner = jnp.sum(probs * dprobs, axis=0, keepdims=True)
                ds = (probs * (dprobs - inner)).astype(LOW)
                dvs.append(mm(probs.astype(LOW), do))
                dks.append(mm(ds, q))
                dqt[pl.ds(pl.multiple_of(base + j * HEAD, HEAD), HEAD), :] = mm(k, ds, 0, 0) * scale
            d_ref[:, pl.ds(pl.multiple_of(2 * width + base, PAIR), PAIR)] = jnp.concatenate(dvs, 1).astype(LOW)
            d_ref[:, pl.ds(pl.multiple_of(width + base, PAIR), PAIR)] = jnp.concatenate(dks, 1).astype(LOW)

    @pl.when(length < slot)
    def _():
        heads(True)

    @pl.when(length >= slot)
    def _():
        heads(False)

    d_ref[:, :width] = dqt[...].T.astype(LOW)
    dtok_ref[...] = (
        mm(d_ref[:, :width], wq[...], 1, 1)
        + mm(d_ref[:, width : 2 * width], wk[...], 1, 1)
        + mm(d_ref[:, 2 * width :], wv[...], 1, 1)
    ).astype(dtok_ref.dtype)


def attend_back(info, saved, do, wq, wk, wv, prev, count, slot):
    q, k, v, lse = saved
    model, width = wq.shape
    full = lambda a: pl.BlockSpec(a.shape, lambda i, s: (0, 0))
    return pl.pallas_call(
        attend_back_kernel,
        grid_spec=pltpu.PrefetchScalarGridSpec(
            num_scalar_prefetch=1,
            grid=(1,),
            in_specs=[full(a) for a in (q, k, v, lse, do, wq, wk, wv)] + [pl.BlockSpec(memory_space=pl.ANY)],
            out_specs=[
                pl.BlockSpec((slot, 3 * width), lambda i, s: (s[0], 0)),
                pl.BlockSpec((slot, model), lambda i, s: (0, 0)),
            ],
            scratch_shapes=[pltpu.VMEM((width, slot), F32)],
        ),
        out_shape=[
            jax.ShapeDtypeStruct((count, 3 * width), LOW),
            jax.ShapeDtypeStruct((slot, model), LOW),
        ],
        input_output_aliases={9: 0},
        cost_estimate=pl.CostEstimate(flops=8 * 10**9, transcendentals=2 * 10**6, bytes_accessed=6 * 10**6),
        name="attend_back",
    )(info, q, k, v, lse, do, wq, wk, wv, prev)


def swap(x, axis, flip):
    size = lax.axis_size(axis)
    return lax.ppermute(x, axis, [(i, i ^ flip) for i in range(size)])


def rows_at(x, start, size):
    return lax.dynamic_slice_in_dim(x, start, size, 0)


def scatter_stage(x, place, low, bits):
    parts = 1 << bits
    share = x.shape[0] // parts
    own = (place >> low) & (parts - 1)
    total = rows_at(x, own * share, share).astype(F32)
    for d in range(1, parts):
        total = total + swap(rows_at(x, (own ^ d) * share, share), "dp", d << low).astype(F32)
    return total.astype(LOW)


def gather_stage(x, place, low, bits):
    parts = 1 << bits
    share = x.shape[0]
    own = (place >> low) & (parts - 1)
    if parts == 2:
        y = swap(x, "dp", 1 << low)
        return jnp.where(own == 0, jnp.concatenate([x, y]), jnp.concatenate([y, x]))
    out = jnp.zeros((share * parts,) + x.shape[1:], x.dtype)
    out = lax.dynamic_update_slice_in_dim(out, x, own * share, 0)
    for d in range(1, parts):
        out = lax.dynamic_update_slice_in_dim(out, swap(x, "dp", d << low), (own ^ d) * share, 0)
    return out


def stages(first, size, most):
    out = []
    while (1 << first) < size:
        bits = 0
        while bits < most and (1 << (first + bits)) < size:
            bits += 1
        out.append((first, bits))
        first += bits
    return out


def sum_over(x, place, plan):
    for low, bits in plan:
        x = scatter_stage(x, place, low, bits)
    return x


def gather_over(x, place, plan):
    for low, bits in reversed(plan):
        x = gather_stage(x, place, low, bits)
    return x


def all_sum(x, place, plan):
    for low, bits in plan:
        total = x
        for d in range(1, 1 << bits):
            total = total + swap(x, "dp", d << low)
        x = total
    return x


def norm(values):
    center = values - jnp.mean(values, axis=-1, keepdims=True)
    root = lax.rsqrt(jnp.mean(center * center, axis=-1, keepdims=True) + 1e-05)
    return center * root, root


def norm_back(grad, n, root):
    return root * (grad - jnp.mean(grad, axis=-1, keepdims=True) - n * jnp.mean(grad * n, axis=-1, keepdims=True))


def gate(u):
    c = 0.7978845608028654
    square = u * u
    t = jnp.tanh(u * (c + (c * 0.044715) * square))
    half = 0.5 + 0.5 * t
    active = u * half
    slope = half + active * (1.0 - t) * (c + (3 * c * 0.044715) * square)
    return active, slope


def shards(
    tokens,
    window_length,
    query_weight,
    query_bias,
    key_weight,
    value_weight,
    value_bias,
    output_weight,
    output_bias,
    first_gain,
    first_shift,
    inner_weight,
    inner_bias,
    outer_weight,
    outer_bias,
    second_gain,
    second_shift,
    cotangent,
):
    count, model = tokens.shape
    windows = window_length.shape[0]
    slot = count // windows
    half = slot // 2
    share = count // 2
    width = query_weight.shape[1]
    m = lax.axis_index("mp")
    place = lax.axis_index("dp")
    dps = lax.axis_size("dp")
    core = place & 1
    cross = lambda x: swap(x, "mp", 1)
    beside = lambda x: swap(x, "dp", 1)
    f32 = lambda x: x.astype(F32)

    wo_half = output_weight.shape[0] // 2
    ff = inner_weight.shape[1] // 2
    wo_part = cross(rows_at(output_weight, core * wo_half, wo_half))
    wo_peer = gather_stage(wo_part, place, 0, 1)
    wi = [lax.dynamic_slice_in_dim(inner_weight, c * ff, ff, 1) for c in (core, 1 - core)]
    wu = [rows_at(outer_weight, c * ff, ff) for c in (core, 1 - core)]
    bi_peer = cross(inner_bias)
    bi = [rows_at(b, c * ff, ff) for b in (inner_bias, bi_peer) for c in (core, 1 - core)]
    hop = 2 if dps > 4 else 1

    def fetch(same, low):
        if dps <= 2:
            return cross(same)
        return gather_stage(cross(rows_at(same, ((place >> low) & 1) * (same.shape[0] // 2), same.shape[0] // 2)), place, low, 1)

    wi.append(fetch(wi[0], 1))
    wu.append(fetch(wu[0], hop))
    wi.append(beside(wi[2]))
    wu.append(beside(wu[2]))

    order = [jnp.where(m == 0, 2 - i, i) for i in range(3)]
    infos = [jnp.stack([w, window_length[w]]) for w in order]
    bq = f32(query_bias)[None]
    bv = f32(value_bias)[None]
    done = [attend(info, tokens, query_weight, key_weight, value_weight, bq, bv, slot) for info in infos]
    mixed = [d[3] for d in done]
    got_win = cross(mixed[0])
    got_half = cross(rows_at(mixed[1], (1 - m) * half, half))
    mix_own = rows_at(jnp.concatenate([mixed[2], mixed[1], mixed[2]]), m * share, share)
    mix_peer = rows_at(jnp.concatenate([got_win, got_half, got_win]), m * slot, share)

    tok_own = f32(rows_at(tokens, m * share, share))
    first_in = tok_own + mm(mix_own, output_weight) + mm(mix_peer, wo_peer) + f32(output_bias)
    n1, root1 = norm(first_in)
    normed = n1 * f32(first_gain) + f32(first_shift)
    low_normed = normed.astype(LOW)
    actives = []
    slopes = []
    second_in = normed + f32(outer_bias)
    for b in range(4):
        a, s = gate(mm(low_normed, wi[b]) + f32(bi[b]))
        actives.append(a.astype(LOW))
        slopes.append(s.astype(LOW))
        second_in = second_in + mm(actives[b], wu[b])
    n2, root2 = norm(second_in)
    layer_out = (n2 * f32(second_gain) + f32(second_shift)).astype(LOW)
    cot = f32(cotangent)
    dsecond = norm_back(cot * f32(second_gain), n2, root2)
    db2 = dsecond.astype(LOW)
    second_ggrad = jnp.sum(cot * n2, axis=0)
    second_sgrad = jnp.sum(cot, axis=0)
    outer_bgrad = jnp.sum(f32(db2), axis=0)
    dnormed = dsecond
    dwi = []
    dwu = []
    dbi = []
    for b in range(4):
        dwu.append(mm(actives[b], db2, 0, 0).astype(LOW))
        dinner = (mm(db2, wu[b], 1, 1) * f32(slopes[b])).astype(LOW)
        dbi.append(jnp.sum(f32(dinner), axis=0))
        dwi.append(mm(low_normed, dinner, 0, 0).astype(LOW))
        dnormed = dnormed + mm(dinner, wi[b], 1, 1)
    first_ggrad = jnp.sum(dnormed * n1, axis=0)
    first_sgrad = jnp.sum(dnormed, axis=0)
    dfirst = norm_back(dnormed * f32(first_gain), n1, root1)
    db1 = dfirst.astype(LOW)
    output_bgrad = jnp.sum(f32(db1), axis=0)
    dmix_own = mm(db1, output_weight, 1, 1).astype(LOW)
    dmix_peer = mm(db1, wo_peer, 1, 1).astype(LOW)
    dwo_own = mm(mix_own, db1, 0, 0).astype(LOW)
    dwo_peer = mm(mix_peer, db1, 0, 0).astype(LOW)

    plan = stages(1, 2, 1) if dps <= 2 else stages(1, dps, 1)
    rest = plan[1:]
    direct = stages(1, 4, 1) + stages(2, dps, 2) if dps > 4 else stages(1, dps, 1)
    u_same = (f32(dwu[0]) + f32(beside(dwu[1]))).astype(LOW)
    u_peer = (f32(dwu[2]) + f32(beside(dwu[3]))).astype(LOW)
    i_both = jnp.concatenate([dwi[0], dwi[2]], 1)
    i_both = (f32(i_both) + f32(beside(jnp.concatenate([dwi[1], dwi[3]], 1)))).astype(LOW)
    u_got = cross(u_peer)
    dmix_own, u_same, i_both = lax.optimization_barrier((dmix_own, u_same, i_both))

    same = lambda x: rows_at(x, core * wo_half, wo_half)
    other = lambda x: rows_at(x, (1 - core) * wo_half, wo_half)
    join = lambda a, b: jnp.where(core == 0, jnp.concatenate([a, b]), jnp.concatenate([b, a]))
    six = jnp.stack([output_bgrad, first_ggrad, first_sgrad, outer_bgrad, second_ggrad, second_sgrad])
    dbi_own = join(dbi[0], dbi[1])
    dbi_own = dbi_own + cross(join(dbi[2], dbi[3]))

    got_dwin = cross(rows_at(dmix_peer, m * half, slot))
    got_dhalf = cross(rows_at(dmix_peer, (1 - m) * slot, half))
    own_dwin = rows_at(dmix_own, m * half, slot)
    own_dhalf = rows_at(dmix_own, (1 - m) * slot, half)
    dmid = rows_at(jnp.concatenate([own_dhalf, got_dhalf, own_dhalf]), m * half, slot)
    grads = jnp.zeros((count, 3 * width), LOW)
    dtok = []
    small_rows = 64
    for role, do in ((2, own_dwin), (1, dmid), (0, got_dwin)):
        if role == 1:
            o_own = (f32(same(dwo_own)) + f32(beside(other(dwo_own)))).astype(LOW)
            o_peer = (f32(same(dwo_peer)) + f32(beside(other(dwo_peer)))).astype(LOW)
            grads, o_own, o_peer = lax.optimization_barrier((grads, o_own, o_peer))
            o_got = cross(o_peer)
            six = six + cross(six)
            six = six + beside(six)
        if role == 0:
            u_sum = (f32(u_same) + f32(u_got)).astype(LOW)
            o_sum = (f32(o_own) + f32(o_got)).astype(LOW)
            tail = jnp.zeros((small_rows - six.shape[0], model), LOW)
            u_all = jnp.concatenate([u_sum, o_sum, six.astype(LOW), tail])
            i_sum = scatter_stage(i_both, place, *plan[0]) if plan else i_both
            grads, u_all, i_sum = lax.optimization_barrier((grads, u_all, i_sum))
        saved = (*done[role][:3], done[role][4])
        grads, dt = attend_back(
            infos[role], saved, do, query_weight, key_weight, value_weight, grads, count, slot
        )
        dtok.append(dt)
    got_thalf = cross(rows_at(dtok[1], (1 - m) * half, half))
    got_twin = cross(dtok[2])
    dtok_own = rows_at(jnp.concatenate([dtok[0], dtok[1], dtok[0]]), m * share, share)
    dtok_peer = rows_at(jnp.concatenate([got_twin, got_thalf, got_twin]), m * slot, share)
    tokens_grad = dfirst + f32(dtok_own) + f32(dtok_peer)

    if plan:
        u_all = scatter_stage(u_all, place, *plan[0])
    if rest:
        i_sum = scatter_stage(i_sum, place, *rest[0])
    dqkv = mm(tokens, grads, 0, 0).astype(LOW)
    dqkv, u_all, i_sum = lax.optimization_barrier((dqkv, u_all, i_sum))
    bias_q = jnp.sum(f32(grads[:, :width]), axis=0)
    bias_v = jnp.sum(f32(grads[:, 2 * width :]), axis=0)
    path = [(0, 1)] + direct
    dqkv = f32(gather_over(sum_over(dqkv, place, path), place, path))

    bias = jnp.concatenate([dbi_own, bias_q, bias_v])
    bias = all_sum(bias.reshape(-1, 128), place, path).reshape(-1)

    u_all = gather_over(sum_over(u_all, place, rest), place, plan)
    i_sum = sum_over(i_sum, place, rest[1:])
    i_sum = (f32(i_sum[:, :ff]) + f32(cross(i_sum[:, ff:]))).astype(LOW)
    i_sum = gather_over(i_sum, place, plan)
    u_red = u_all[:ff]
    o_red = u_all[ff : ff + wo_half]
    six = f32(u_all[ff + wo_half : ff + wo_half + 6])
    u_beside = beside(u_all)
    i_beside = beside(i_sum)
    outer_wgrad = f32(join(u_red, u_beside[:ff]))
    output_wgrad = f32(join(o_red, u_beside[ff : ff + wo_half]))
    inner_wgrad = f32(
        jnp.where(core == 0, jnp.concatenate([i_sum, i_beside], 1), jnp.concatenate([i_beside, i_sum], 1))
    )
    return (
        layer_out,
        tokens_grad,
        dqkv[:, :width],
        bias[2 * ff : 2 * ff + width],
        dqkv[:, width : 2 * width],
        dqkv[:, 2 * width :],
        bias[2 * ff + width :],
        output_wgrad,
        six[0],
        six[1],
        six[2],
        inner_wgrad,
        bias[: 2 * ff],
        outer_wgrad,
        six[3],
        six[4],
        six[5],
    )


def solution(mesh):
    in_specs = (
        P("dp", None),
        P("dp"),
        P(None, "mp"),
        P("mp"),
        P(None, "mp"),
        P(None, "mp"),
        P("mp"),
        P("mp", None),
        P(),
        P(),
        P(),
        P(None, "mp"),
        P("mp"),
        P("mp", None),
        P(),
        P(),
        P(),
        P(("dp", "mp"), None),
    )
    out_specs = (
        P(("dp", "mp"), None),
        P(("dp", "mp"), None),
        P(None, "mp"),
        P("mp"),
        P(None, "mp"),
        P(None, "mp"),
        P("mp"),
        P("mp", None),
        P(),
        P(),
        P(),
        P(None, "mp"),
        P("mp"),
        P("mp", None),
        P(),
        P(),
        P(),
    )
    return jax.shard_map(shards, mesh=mesh, in_specs=in_specs, out_specs=out_specs, check_vma=False)
```
